32 devices in a mesh: rows: 8 (over z, y), seq: 4 (over x, core).
Axes of the slice: x: 2, y: 2, z: 4, core: 2. Of those that a mesh axis runs over, the one named last changes fastest.
Arguments:
- molecules: bfloat16 [16, 512, 768], P('rows', 'seq'), may hold values from -6 to 6
- norm_gain: bfloat16 [768], P(('rows', 'seq')), may hold values from 0.5 to 1.5
- norm_shift: bfloat16 [768], P(('rows', 'seq')), may hold values from -3 to 3
- query_weight: bfloat16 [768, 768], P(('rows', 'seq')), may hold values from -0.21875 to 0.21875
- query_bias: bfloat16 [768], P(('rows', 'seq')), may hold values from -3 to 3
- key_weight: bfloat16 [768, 768], P(('rows', 'seq')), may hold values from -0.21875 to 0.21875
- value_weight: bfloat16 [768, 768], P(('rows', 'seq')), may hold values from -0.21875 to 0.21875
- value_bias: bfloat16 [768], P(('rows', 'seq')), may hold values from -3 to 3
- output_weight: bfloat16 [768, 768], P(('rows', 'seq')), may hold values from -0.625 to 0.625
- output_bias: bfloat16 [768], P(('rows', 'seq')), may hold values from -3 to 3
- middle_gain: bfloat16 [768], P(('rows', 'seq')), may hold values from 0.5 to 1.5
- middle_shift: bfloat16 [768], P(('rows', 'seq')), may hold values from -3 to 3
- up_weight: bfloat16 [768, 3072], P(('rows', 'seq')), may hold values from -0.21875 to 0.21875
- up_bias: bfloat16 [3072], P(('rows', 'seq')), may hold values from -3 to 3
- down_weight: bfloat16 [3072, 768], P(('rows', 'seq')), may hold values from -0.109375 to 0.109375
- down_bias: bfloat16 [768], P(('rows', 'seq')), may hold values from -3 to 3
- cotangent: bfloat16 [16, 512, 768], P('rows', 'seq'), may hold values from -6 to 6
- lengths: int32 [16], P('rows'), may hold values from 200 to 2048, as said below
- codepoints: int32 [16, 2048], P('rows', 'seq'), may hold values from 0 to 65535
Outputs:
- layer_out: bfloat16 [16, 512, 768], P('rows', 'seq')
- input_grad: bfloat16 [16, 512, 768], P('rows', 'seq')
- norm_gain_grad: float32 [768], P(('rows', 'seq'))
- norm_shift_grad: float32 [768], P(('rows', 'seq'))
- query_weight_grad: float32 [768, 768], P(('rows', 'seq'))
- query_bias_grad: float32 [768], P(('rows', 'seq'))
- key_weight_grad: float32 [768, 768], P(('rows', 'seq'))
- value_weight_grad: float32 [768, 768], P(('rows', 'seq'))
- value_bias_grad: float32 [768], P(('rows', 'seq'))
- output_weight_grad: float32 [768, 768], P(('rows', 'seq'))
- output_bias_grad: float32 [768], P(('rows', 'seq'))
- middle_gain_grad: float32 [768], P(('rows', 'seq'))
- middle_shift_grad: float32 [768], P(('rows', 'seq'))
- up_weight_grad: float32 [768, 3072], P(('rows', 'seq'))
- up_bias_grad: float32 [3072], P(('rows', 'seq'))
- down_weight_grad: float32 [3072, 768], P(('rows', 'seq'))
- down_bias_grad: float32 [768], P(('rows', 'seq'))
- bucket_counts: int32 [8, 16384], replicated
The draws below stay inside these ranges and needn't reach their ends.
Inputs may be any that keep to these rules, and one draw needn't show every extreme that they name: `lengths`: every text has at least 200 and at most 2048 characters; some text has exactly 200 and some exactly 2048.
All inputs are finite; a program needn't handle non-finite values.
Results may differ from the reference program's by a relative error of at most 0.015.
Values may be sent and summed in bfloat16 or wider, within the bound.
No kernel may reach another device: no remote copies, remote signals or barrier semaphores. Data moves between devices by JAX's collectives and lax.ppermute only.
A program may use at most 128 MiB of HBM per device.

```python
import math
import jax
import jax.numpy as jnp
import numpy as np
from jax import lax

D = 768
HEAD_DIM = 64
FF = 3072
HASHES = 8
BUCKETS = 16384
MOL = 512
RATE = 4
CHARS = 2048
MIN_LEN = 200
TEXTS = 16


def draw_lengths(key, part):
    drawn = jax.random.randint(key, (TEXTS,), MIN_LEN, CHARS + 1, dtype=jnp.int32)
    return drawn.at[0].set(CHARS).at[1].set(MIN_LEN)


def set_ends(values, key, least, high):
    longest = values.shape.index(max(values.shape))
    spots = []
    for shift in (0, 1):
        where = [jax.random.randint(jax.random.fold_in(key, axis), (), 0, length) for axis, length in enumerate(values.shape)]
        where[longest] = (where[longest] + shift) % values.shape[longest]
        spots.append(tuple(where))
    return values.at[spots[0]].set(least).at[spots[1]].set(high)


def spiked(values, own_key, source, target, parts, factor):
    owner, partner = [(jnp.arange(values.shape[dim]) // (values.shape[dim] // parts)).reshape([-1 if axis == dim else 1 for axis in range(values.ndim)]) for dim in (source, target)]
    chosen = jax.random.permutation(own_key, parts)[partner]
    strong = (owner == chosen) | (owner == (partner + parts // 2) % parts)
    return jnp.where(strong, factor * values, values)


def shard_levels(stream_key, shape, cuts, smallest, high):
    factor_of, own = 1.0, jax.random.fold_in(stream_key, 6)
    for position, shards_of in cuts:
        steps = jnp.exp(jax.random.uniform(jax.random.fold_in(own, position), (shards_of,), jnp.float32, smallest / len(cuts), high / len(cuts)))
        factor_of = factor_of * jnp.repeat(steps, shape[position] // shards_of).reshape([-1 if axis == position else 1 for axis in range(len(shape))])
    return factor_of


def rank_table(number_of, lean):
    loads = [(1 << 20) // math.isqrt(standing ** lean) + 1 for standing in range(1, number_of + 1)]
    scale = 1 + sum(loads) // (1 << 30)
    return np.cumsum(np.array([max(1, weight // scale) for weight in loads]))


def skewed_ids(rng, shape, amount, slope):
    table = rank_table(amount, slope)
    lot = jax.random.randint(jax.random.fold_in(rng, 1), shape, 0, int(table[amount - 1]))
    standing = jnp.searchsorted(jnp.asarray(table, jnp.int32), lot, side="right")
    return jax.random.permutation(jax.random.fold_in(rng, 2), amount)[standing].astype(jnp.int32)


def normal_values(key, extent, deviation, limit, cuts=(), kind=jnp.bfloat16):
    level = shard_levels(key, extent, cuts, -0.22, 0.18) if cuts else 1.0
    values = jax.random.normal(key, extent, jnp.float32) * deviation * level
    return jnp.minimum(jnp.maximum(values, -limit), limit).astype(kind)


def gaussian_with(stream_key, extent, deviation, most, cuts, heavy, held_as=jnp.bfloat16):
    values = deviation * jax.random.normal(stream_key, extent, jnp.float32)
    if cuts:
        values = values * shard_levels(stream_key, extent, cuts, -0.22, 0.18)
    return jnp.clip(spiked(values, jax.random.fold_in(stream_key, 3), *heavy), -most, most).astype(held_as)


def setup_inputs(seed: int = 0) -> dict:
    key_of = jax.random.split(jax.random.key(seed), 20)
    return {
        "molecules": normal_values(key_of[0], (TEXTS, MOL, D), 1.0, 6.0, ((0, 8), (1, 4))),
        "norm_gain": jnp.clip(1.0 + 0.1 * jax.random.normal(key_of[1], (D,), jnp.float32), 0.5, 1.5).astype(jnp.bfloat16),
        "norm_shift": normal_values(key_of[2], (D,), 0.5, 3.0, ((0, 32),)),
        "query_weight": normal_values(key_of[3], (D, D), D ** -0.5, 0.21875, ((0, 32),)),
        "query_bias": normal_values(key_of[4], (D,), 0.5, 3.0, ((0, 32),)),
        "key_weight": normal_values(key_of[5], (D, D), D ** -0.5, 0.21875, ((0, 32),)),
        "value_weight": normal_values(key_of[6], (D, D), D ** -0.5, 0.21875, ((0, 32),)),
        "value_bias": normal_values(key_of[7], (D,), 0.5, 3.0, ((0, 32),)),
        "output_weight": normal_values(key_of[8], (D, D), (D // 8) ** -0.5, 0.625, ((0, 32),)),
        "output_bias": normal_values(key_of[9], (D,), 0.5, 3.0, ((0, 32),)),
        "middle_gain": jnp.clip(1.0 + 0.1 * jax.random.normal(key_of[10], (D,), jnp.float32), 0.5, 1.5).astype(jnp.bfloat16),
        "middle_shift": normal_values(key_of[11], (D,), 0.5, 3.0, ((0, 32),)),
        "up_weight": normal_values(key_of[12], (D, FF), D ** -0.5, 0.21875, ((0, 32),)),
        "up_bias": normal_values(key_of[13], (FF,), 0.5, 3.0, ((0, 32),)),
        "down_weight": normal_values(key_of[14], (FF, D), FF ** -0.5, 0.109375, ((0, 32),)),
        "down_bias": normal_values(key_of[15], (D,), 0.5, 3.0, ((0, 32),)),
        "cotangent": gaussian_with(key_of[16], (TEXTS, MOL, D), 1.0, 6.0, ((0, 8), (1, 4)), (0, 2, 8, 2.0)),
        "lengths": draw_lengths(jax.random.fold_in(key_of[19], 71), 0),
        "codepoints": set_ends(skewed_ids(key_of[18], (TEXTS, CHARS), 65536, 2), jax.random.fold_in(key_of[18], 3), 0, 65535).astype(jnp.int32),
    }


hash_primes = (31, 43, 59, 61, 73, 97, 103, 113)
epsilon = 1e-05
masked_score = -1000000000.0

@jax.custom_vjp
def low(v):
    return lax.optimization_barrier(v.astype(jnp.bfloat16)).astype(jnp.float32)

@jax.custom_vjp
def low_back(v):
    return v

def low_keep(v):
    return (low(v), None)

def low_pass(kept, grad):
    return (grad,)

def back_keep(v):
    return (v, None)

def back_low(kept, grad):
    return (low(grad),)
low.defvjp(low_keep, low_pass)
low_back.defvjp(back_keep, back_low)

def normalize(values, gain, shift):
    center = values - lax.optimization_barrier(jnp.mean(values, axis=-1, keepdims=True))
    spread = lax.optimization_barrier(jnp.mean(center * center, axis=-1, keepdims=True))
    return center * lax.rsqrt(spread + epsilon) * gain + shift

def project(values, matrix):
    return jnp.einsum('gmd,de->gme', values, matrix, precision=lax.Precision.HIGHEST)

def layer_forward(params, block, key_valid):
    norm_gain, norm_shift, query_weight, query_bias, key_weight, value_weight, value_bias, output_weight, output_bias, middle_gain, middle_shift, up_weight, up_bias, down_weight, down_bias = params
    groups, length, width = block.shape
    heads = width // HEAD_DIM
    normed = low(normalize(block, norm_gain, norm_shift))
    query = low_back(low(project(normed, query_weight) + query_bias)).reshape(groups, length, heads, HEAD_DIM)
    keys = low_back(low(project(normed, key_weight))).reshape(groups, length, heads, HEAD_DIM)
    vals = low_back(low(project(normed, value_weight) + value_bias)).reshape(groups, length, heads, HEAD_DIM)
    scores = low_back(jnp.einsum('gqhd,gkhd->ghqk', query, keys, precision=lax.Precision.HIGHEST) * HEAD_DIM ** (-0.5))
    scores = jnp.where(key_valid[:, None, None, :], scores, masked_score)
    top = lax.optimization_barrier(jnp.max(scores, axis=-1, keepdims=True))
    expo = jnp.exp(scores - top)
    probs = low(expo / lax.optimization_barrier(jnp.sum(expo, axis=-1, keepdims=True)))
    mixed = jnp.einsum('ghqk,gkhd->gqhd', probs, vals, precision=lax.Precision.HIGHEST)
    mixed = low_back(low(mixed.reshape(groups, length, width)))
    middle = block + low_back(project(mixed, output_weight) + output_bias)
    normed_two = low(normalize(middle, middle_gain, middle_shift))
    inner = low_back(project(normed_two, up_weight) + up_bias)
    active = low(jax.nn.gelu(inner, approximate=False))
    return middle + low_back(project(active, down_weight) + down_bias)

def reference(molecules, norm_gain, norm_shift, query_weight, query_bias, key_weight, value_weight, value_bias, output_weight, output_bias, middle_gain, middle_shift, up_weight, up_bias, down_weight, down_bias, cotangent, lengths, codepoints):
    params = tuple((p.astype(jnp.float32) for p in (norm_gain, norm_shift, query_weight, query_bias, key_weight, value_weight, value_bias, output_weight, output_bias, middle_gain, middle_shift, up_weight, up_bias, down_weight, down_bias)))
    texts, length, width = molecules.shape
    group = math.gcd(texts, max(1, 4096 // length))
    steps_count = texts // group
    live_molecules = (lengths + RATE - 1) // RATE
    key_valid = jnp.arange(length, dtype=jnp.int32)[None, :] < live_molecules[:, None]
    blocks = molecules.astype(jnp.float32).reshape(steps_count, group, length, width)
    tangents = cotangent.astype(jnp.float32).reshape(steps_count, group, length, width)
    valids = key_valid.reshape(steps_count, group, length)

    def step(totals, pieces):
        block, tangent, valid = pieces
        result, pullback = jax.vjp(lambda p, b: layer_forward(p, b, valid), params, block)
        param_grads, block_grad = pullback(tangent)
        totals = jax.tree.map(jnp.add, totals, param_grads)
        return (totals, (result.astype(jnp.bfloat16), block_grad.astype(jnp.bfloat16)))
    zeros = tuple((jnp.zeros(p.shape, jnp.float32) for p in params))
    totals, (outputs, grads) = lax.scan(step, zeros, (blocks, tangents, valids))
    layer_out = outputs.reshape(texts, length, width)
    input_grad = grads.reshape(texts, length, width)
    positions = jnp.arange(CHARS, dtype=jnp.int32)
    live = (positions[None, :] < lengths[:, None]).astype(jnp.int32)
    primes = jnp.array(hash_primes, jnp.int32)[:HASHES]
    buckets = (codepoints[None, :, :] + 1) * primes[:, None, None] % BUCKETS
    which = jnp.broadcast_to(jnp.arange(HASHES, dtype=jnp.int32)[:, None, None], buckets.shape)
    weights = jnp.broadcast_to(live[None, :, :], buckets.shape)
    counts = jnp.zeros((HASHES, BUCKETS), jnp.int32).at[which, buckets].add(weights)
    return (layer_out, input_grad, totals[0], totals[1], totals[2], totals[3], totals[4], totals[5], totals[6], totals[7], totals[8], totals[9], totals[10], totals[11], totals[12], totals[13], totals[14], counts)
```

```python
import functools

import jax
import jax.numpy as jnp
import numpy as np
from jax import lax
from jax.experimental import pallas as pl
from jax.experimental.pallas import tpu as pltpu
from jax.sharding import PartitionSpec as P

HEAD_DIM = 64
HASHES = 8
BUCKETS = 16384
SIDE = 128
RATE = 4
AXES = ("rows", "seq")

hash_primes = (31, 43, 59, 61, 73, 97, 103, 113)
epsilon = 1e-05
masked_score = -1000000000.0
bf16, f32 = jnp.bfloat16, jnp.float32


def normalize(values, gain, shift):
    center = values - jnp.mean(values, axis=-1, keepdims=True)
    inverse = lax.rsqrt(jnp.mean(center * center, axis=-1, keepdims=True) + epsilon)
    scaled = center * inverse
    return (scaled * gain + shift, scaled, inverse)


def normalize_back(grad_out, scaled, inverse, gain):
    grad_scaled = grad_out * gain
    inner = grad_scaled - jnp.mean(grad_scaled, axis=-1, keepdims=True)
    inner = inner - scaled * jnp.mean(grad_scaled * scaled, axis=-1, keepdims=True)
    return (inner * inverse, jnp.sum(grad_out * scaled, axis=0), jnp.sum(grad_out, axis=0))


def linear(left, right):
    return jnp.dot(left, right, preferred_element_type=f32)


def linear_back(left, right):
    return lax.dot_general(left, right, (((1,), (1,)), ((), ())), preferred_element_type=f32)


def outer_sum(left, right):
    return lax.dot_general(left, right, (((0,), (0,)), ((), ())), preferred_element_type=f32)


def column_sum(values):
    return jnp.sum(values.astype(f32), axis=0)


def gelu_both(inner):
    cumul = 0.5 * (1.0 + lax.erf(inner * 0.7071067811865476))
    density = jnp.exp(-0.5 * inner * inner) * 0.3989422804014327
    return (inner * cumul, cumul + inner * density)


def swap(values, bit, devices):
    return lax.ppermute(values, AXES, [(i, i ^ bit) for i in range(devices)])


def halve(blocks, bit, low, devices, me):
    count, rows, width = blocks.shape
    step = bit // low
    view = blocks.reshape(count // (2 * step), 2, step, rows, width)
    mine = (me // bit) % 2
    send = lax.dynamic_index_in_dim(view, 1 - mine, 1, keepdims=False)
    keep = lax.dynamic_index_in_dim(view, mine, 1, keepdims=False)
    got = swap(send.reshape(count // 2, rows, width).astype(bf16), bit, devices)
    return keep.reshape(count // 2, rows, width).astype(f32) + got.astype(f32)


def reduce_blocks(first, second, devices, me):
    both = halve(jnp.concatenate([first, second], axis=1), 1, 1, devices, me).astype(bf16)
    cut = first.shape[1]
    first, second = both[:, :cut], both[:, cut:]
    bits = [1 << k for k in range(1, devices.bit_length() - 1)]
    a, b = bits[0], bits[1]
    first = halve(first, a, 2, devices, me).astype(bf16)
    second = halve(second, b, 2, devices, me).astype(bf16)
    first = halve(first, b, b, devices, me).astype(bf16)
    second = halve(second, a, 2, devices, me).astype(bf16)
    both = jnp.concatenate([first, second], axis=1)
    for bit in bits[2:]:
        both = halve(both, bit, bit, devices, me)
        if bit != bits[-1]:
            both = both.astype(bf16)
    return both[0]


@functools.lru_cache(None)
def hash_tables():
    spot = np.arange(SIDE)
    rows, columns, turns = [], [], []
    for prime in hash_primes:
        rows.append(np.eye(SIDE, dtype=np.float32)[(spot * prime) % SIDE].T)
        columns.append(np.eye(SIDE, dtype=np.float32)[(spot * prime) % SIDE])
        turn = np.zeros(SIDE, np.int32)
        turn[(spot * prime) % SIDE] = (spot * prime) // SIDE
        turns.append(turn)
    return np.stack(rows), np.stack(columns), np.stack(turns)


def counts_kernel(high_ref, low_ref, row_ref, column_ref, turn_ref, out_ref, total):
    step = pl.program_id(0)

    @pl.when(step == 0)
    def _():
        total[...] = jnp.zeros_like(total)

    spot = lax.broadcasted_iota(jnp.int32, (SIDE, high_ref.shape[1]), 0).astype(f32)
    acc = total[...]
    for line in range(high_ref.shape[0]):
        high = (spot == high_ref[line : line + 1, :].astype(f32)).astype(bf16)
        low = (spot == low_ref[line : line + 1, :].astype(f32)).astype(bf16)
        acc = acc + lax.dot_general(high, low, (((1,), (1,)), ((), ())), preferred_element_type=f32)
    total[...] = acc

    @pl.when(step == pl.num_programs(0) - 1)
    def _():
        base = total[...]
        for which in range(HASHES):
            moved = jnp.dot(row_ref[which], base, precision=lax.Precision.HIGHEST, preferred_element_type=f32)
            moved = jnp.dot(moved, column_ref[which], precision=lax.Precision.HIGHEST, preferred_element_type=f32)
            turn = turn_ref[which : which + 1, :]
            for k in range(7):
                turned = pltpu.roll(moved, 1 << k, 0)
                moved = jnp.where((turn >> k) & 1 == 1, turned, moved)
            out_ref[which] = moved.astype(jnp.int32)


def bucket_counts(high, low):
    lines, width = high.shape
    tile = 16
    rows, columns, turns = hash_tables()
    out = pl.pallas_call(
        counts_kernel,
        grid=(lines // tile,),
        in_specs=[
            pl.BlockSpec((tile, width), lambda i: (i, 0)),
            pl.BlockSpec((tile, width), lambda i: (i, 0)),
            pl.BlockSpec((HASHES, SIDE, SIDE), lambda i: (0, 0, 0)),
            pl.BlockSpec((HASHES, SIDE, SIDE), lambda i: (0, 0, 0)),
            pl.BlockSpec((HASHES, SIDE), lambda i: (0, 0)),
        ],
        out_specs=pl.BlockSpec((HASHES, SIDE, SIDE), lambda i: (0, 0, 0)),
        out_shape=jax.ShapeDtypeStruct((HASHES, SIDE, SIDE), jnp.int32),
        scratch_shapes=[pltpu.VMEM((SIDE, SIDE), f32)],
        name="counts",
    )(high, low, jnp.asarray(rows), jnp.asarray(columns), jnp.asarray(turns))
    return out.reshape(HASHES, BUCKETS)


def body(
    devices,
    molecules,
    norm_gain,
    norm_shift,
    query_weight,
    query_bias,
    key_weight,
    value_weight,
    value_bias,
    output_weight,
    output_bias,
    middle_gain,
    middle_shift,
    up_weight,
    up_bias,
    down_weight,
    down_bias,
    cotangent,
    lengths,
    codepoints,
):
    texts, local_len, width = molecules.shape
    hidden = up_weight.shape[1]
    part = query_weight.shape[0]
    wide = hidden // width
    seq = lax.axis_index("seq")
    seq_size = lax.axis_size("seq")
    me = lax.axis_index("rows") * seq_size + seq

    local_chars = codepoints.shape[1]
    position = seq * local_chars + jnp.arange(local_chars, dtype=jnp.int32)
    live = position[None, :] < lengths[:, None]
    base = (codepoints + 1) % BUCKETS
    digits = jnp.concatenate([jnp.where(live, base // SIDE, -1), base % SIDE], axis=0).astype(bf16)
    digits = jnp.pad(digits, ((0, 0), (0, width - local_chars)))

    shares = jnp.stack(
        [norm_gain, norm_shift, query_bias, value_bias, output_bias, middle_gain, middle_shift, down_bias]
    )
    lines = lax.dynamic_update_slice(jnp.zeros((8, width), bf16), shares, (0, me * part))
    up_line = lax.dynamic_update_slice(jnp.zeros((hidden,), bf16), up_bias, (me * (hidden // devices),))
    sent = jnp.concatenate(
        [query_weight, key_weight, value_weight, output_weight]
        + [up_weight[:, k * width : (k + 1) * width] for k in range(wide)]
        + [down_weight, lines, up_line.reshape(wide, width), digits],
        axis=0,
    )
    got = lax.all_gather(sent, AXES, axis=0, tiled=False)

    def piece(at, rows):
        return got[:, at : at + rows].reshape(devices * rows, width)

    query_mat, key_mat, value_mat, output_mat = (piece(k * part, part) for k in range(4))
    up_mat = jnp.concatenate([piece((4 + k) * part, part) for k in range(wide)], axis=1)
    at = (4 + wide) * part
    down_rows = down_weight.shape[0]
    down_mat = piece(at, down_rows)
    at += down_rows
    vectors = jnp.sum(got[:, at : at + 8 + wide].astype(f32), axis=0)
    gain_first, shift_first, query_add, value_add, output_add, gain_second, shift_second, down_add = (
        vectors[k] for k in range(8)
    )
    up_add = vectors[8 : 8 + wide].reshape(hidden)
    at += 8 + wide
    counts = bucket_counts(
        got[:, at : at + texts, :local_chars].reshape(devices * texts, local_chars),
        got[:, at + texts : at + 2 * texts, :local_chars].reshape(devices * texts, local_chars),
    )

    everyone = molecules
    bit = 1
    while bit < seq_size:
        everyone = jnp.concatenate([everyone, swap(everyone, bit, devices)], axis=1)
        bit *= 2
    total_len = everyone.shape[1]
    rows = texts * local_len
    heads = width // HEAD_DIM
    scale = HEAD_DIM ** (-0.5)
    normed_all, scaled_all, inverse_all = normalize(everyone.astype(f32), gain_first, shift_first)
    all_low = normed_all.astype(bf16)
    normed_low = all_low[:, :local_len].reshape(rows, width)
    scaled_one = scaled_all[:, :local_len].reshape(rows, width)
    inverse_one = inverse_all[:, :local_len].reshape(rows, 1)
    all_low = all_low.reshape(texts * total_len, width)
    flat = molecules.reshape(rows, width).astype(f32)

    query_low = (linear(normed_low, query_mat) + query_add).astype(bf16)
    key_low = linear(all_low, key_mat).astype(bf16)
    value_low = (linear(all_low, value_mat) + value_add).astype(bf16)
    block = jnp.arange(seq_size, dtype=jnp.int32)
    where = ((seq ^ block)[:, None] * local_len + jnp.arange(local_len, dtype=jnp.int32)[None, :]).reshape(-1)
    key_valid = where[None, :] < ((lengths + RATE - 1) // RATE)[:, None]
    query_heads = query_low.reshape(texts, local_len, heads, HEAD_DIM)
    key_heads = key_low.reshape(texts, total_len, heads, HEAD_DIM)
    value_heads = value_low.reshape(texts, total_len, heads, HEAD_DIM)

    raw = jnp.einsum("tqhd,tkhd->thqk", query_heads, key_heads, preferred_element_type=f32) * scale
    scores = jnp.where(key_valid[:, None, None, :], raw, masked_score)
    top = jnp.max(scores, axis=-1, keepdims=True)
    expo = jnp.exp(scores - top)
    total = jnp.sum(expo, axis=-1, keepdims=True)
    probs = expo / total
    probs_low = probs.astype(bf16)
    mixed = jnp.einsum("thqk,tkhd->tqhd", probs_low, value_heads, preferred_element_type=f32)
    mixed_low = mixed.reshape(rows, width).astype(bf16)
    middle = flat + linear(mixed_low, output_mat) + output_add
    normed_two, scaled_two, inverse_two = normalize(middle, gain_second, shift_second)
    normed_two_low = normed_two.astype(bf16)
    inner = linear(normed_two_low, up_mat) + up_add
    active, slope = gelu_both(inner)
    active_low = active.astype(bf16)
    result = middle + linear(active_low, down_mat) + down_add
    layer_out = result.astype(bf16).reshape(texts, local_len, width)
    grad_out = cotangent.reshape(rows, width)
    grad_out_wide = grad_out.astype(f32)
    down_add_grad = column_sum(grad_out)
    down_mat_grad = outer_sum(active_low, grad_out).astype(bf16)
    grad_active = linear_back(grad_out, down_mat)
    grad_inner_low = (grad_active * slope).astype(bf16)
    up_add_grad = column_sum(grad_inner_low)
    up_mat_grad = outer_sum(normed_two_low, grad_inner_low).astype(bf16)

    def parts(grad):
        return grad.reshape(devices, grad.shape[0] // devices, width)

    feed = reduce_blocks(
        jnp.concatenate([parts(up_mat_grad[:, k * width : (k + 1) * width]) for k in range(wide)], axis=1),
        parts(down_mat_grad),
        devices,
        me,
    )
    grad_normed_two = linear_back(grad_inner_low, up_mat)
    middle_part, gain_second_grad, shift_second_grad = normalize_back(
        grad_normed_two, scaled_two, inverse_two, gain_second
    )
    grad_middle = grad_out_wide + middle_part
    grad_branch_low = grad_middle.astype(bf16)
    output_add_grad = column_sum(grad_branch_low)
    output_mat_grad = outer_sum(mixed_low, grad_branch_low).astype(bf16)
    grad_mixed_low = linear_back(grad_branch_low, output_mat).astype(bf16)
    grad_heads = grad_mixed_low.reshape(texts, local_len, heads, HEAD_DIM)
    grad_probs = jnp.einsum("tqhd,tkhd->thqk", grad_heads, value_heads, preferred_element_type=f32)
    delta = jnp.sum(grad_probs * probs, axis=-1, keepdims=True)
    grad_scores_low = (probs * (grad_probs - delta)).astype(bf16)
    grad_query = jnp.einsum("thqk,tkhd->tqhd", grad_scores_low, key_heads, preferred_element_type=f32) * scale
    key_part = jnp.einsum("thqk,tqhd->tkhd", grad_scores_low, query_heads, preferred_element_type=f32) * scale
    value_part = jnp.einsum("thqk,tqhd->tkhd", probs_low, grad_heads, preferred_element_type=f32)
    grad_query_low = grad_query.reshape(rows, width).astype(bf16)
    key_part_low = key_part.reshape(texts * total_len, width).astype(bf16)
    value_part_low = value_part.reshape(texts * total_len, width).astype(bf16)
    query_add_grad = column_sum(grad_query_low)
    value_add_grad = column_sum(value_part_low)
    query_mat_grad = outer_sum(normed_low, grad_query_low).astype(bf16)
    key_mat_grad = outer_sum(all_low, key_part_low).astype(bf16)
    value_mat_grad = outer_sum(all_low, value_part_low).astype(bf16)
    shared = linear_back(key_part_low, key_mat) + linear_back(value_part_low, value_mat)
    shared = shared.reshape(texts, total_len, width)
    bit = seq_size // 2
    while bit:
        cut = bit * local_len
        shared = shared[:, :cut] + swap(shared[:, cut:].astype(bf16), bit, devices).astype(f32)
        bit //= 2
    grad_normed = linear_back(grad_query_low, query_mat) + shared.reshape(rows, width)
    input_part, gain_first_grad, shift_first_grad = normalize_back(
        grad_normed, scaled_one, inverse_one, gain_first
    )
    input_grad = (grad_middle + input_part).astype(bf16).reshape(texts, local_len, width)
    vector_grads = jnp.stack(
        [
            gain_first_grad,
            shift_first_grad,
            query_add_grad,
            value_add_grad,
            output_add_grad,
            gain_second_grad,
            shift_second_grad,
            down_add_grad,
        ]
    ).astype(bf16)
    vector_parts = jnp.moveaxis(vector_grads.reshape(8, devices, part), 1, 0).reshape(devices, 8 * part)
    up_parts = up_add_grad.astype(bf16).reshape(devices, hidden // devices)
    used = 8 * part + hidden // devices
    line = jnp.pad(jnp.concatenate([vector_parts, up_parts], axis=1), ((0, 0), (0, width - used)))
    line = jnp.pad(line[:, None, :], ((0, 0), (0, 7), (0, 0)))
    attention = reduce_blocks(
        jnp.concatenate([parts(query_mat_grad), parts(key_mat_grad)], axis=1),
        jnp.concatenate([parts(value_mat_grad), parts(output_mat_grad), line], axis=1),
        devices,
        me,
    )
    small = attention[4 * part]
    vector_out = [small[k * part : (k + 1) * part] for k in range(8)]
    up_out = small[8 * part : used]
    up_grad = jnp.concatenate([feed[k * part : (k + 1) * part] for k in range(wide)], axis=1)
    down_grad = feed[wide * part :]
    return (
        layer_out,
        input_grad,
        vector_out[0],
        vector_out[1],
        attention[:part],
        vector_out[2],
        attention[part : 2 * part],
        attention[2 * part : 3 * part],
        vector_out[3],
        attention[3 * part : 4 * part],
        vector_out[4],
        vector_out[5],
        vector_out[6],
        up_grad,
        up_out,
        down_grad,
        vector_out[7],
        counts,
    )


def solution(mesh):
    both = P(("rows", "seq"))
    flat2 = P(("rows", "seq"), None)
    tokens = P("rows", "seq", None)
    devices = mesh.shape["rows"] * mesh.shape["seq"]
    return jax.shard_map(
        functools.partial(body, devices),
        mesh=mesh,
        in_specs=(
            tokens, both, both, flat2, both, flat2, flat2, both, flat2, both,
            both, both, flat2, both, flat2, both, tokens, P("rows"), P("rows", "seq"),
        ),
        out_specs=(
            tokens, tokens, both, both, flat2, both, flat2, flat2, both, flat2,
            both, both, both, flat2, both, flat2, both, P(),
        ),
        check_vma=False,
    )
```
